256 devices in a mesh: dp: 8 (over z_lo, core), heads: 32 (over y, x, z_hi).
Axes of the slice: x: 4, y: 4, z: 8 (z_hi: 2, z_lo: 4; z = z_hi * 4 + z_lo), core: 2. Of those that a mesh axis runs over, the one named last changes fastest.
Arguments:
- latent: bfloat16 [8, 1024, 512], P(None, 'dp'), may hold values from -6 to 6
- rope_keys: bfloat16 [8, 1024, 64], P(None, 'dp'), may hold values from -6 to 6
- queries: bfloat16 [8, 1024, 24576], P(None, 'dp', 'heads'), may hold values from -320 to 320
- grad_out: bfloat16 [8, 1024, 16384], P(None, 'dp', 'heads'), may hold values from -2 to 2
- key_value_up_weight: bfloat16 [8, 512, 32768], P('dp', None, 'heads'), may hold values from -0.25 to 0.25
- momentum: bfloat16 [8, 512, 32768], P('dp', None, 'heads'), may hold values from -16 to 16
Outputs:
- new_momentum: bfloat16 [8, 512, 32768], P('dp', None, 'heads')
- layer_update_step: float32 [8, 512, 32768], P('dp', None, 'heads')
The draws below stay inside these ranges and needn't reach their ends.
All inputs are finite; a program needn't handle non-finite values.
Results may differ from the reference program's by a relative error of at most 0.015.
Values may be sent and summed in bfloat16 or wider, within the bound.
No kernel may reach another device: no remote copies, remote signals or barrier semaphores. Data moves between devices by JAX's collectives and lax.ppermute only.
A program may use at most 64 MiB of HBM per device.

```python
import math
import jax
import jax.numpy as jnp
from jax import lax

LATENT = 512
HEADS = 128
NOPE = 128
ROPE = 64
VDIM = 128
SEQ = 128
STEPS = 2
LAYERS = 8
TOKENS = 1024
COLS = 32768
N_DP = 8


def shared_rope(key):
    base = jax.random.normal(jax.random.fold_in(key, 101), (LAYERS, TOKENS, ROPE), jnp.float32)
    return jnp.clip(base, -6.0, 6.0)


def draw_rope_keys(key, part):
    return shared_rope(key).astype(jnp.bfloat16)


def draw_queries(key, part):
    width = NOPE + ROPE
    shape = (LAYERS, TOKENS, HEADS, width)
    values = jnp.clip(jax.random.normal(jax.random.fold_in(key, 202), shape, jnp.float32), -6.0, 6.0)
    return values.reshape(LAYERS, TOKENS, HEADS * width).astype(jnp.bfloat16)


def head_ramp(key, ratio):
    position = jnp.arange(HEADS, dtype=jnp.float32) / max(HEADS - 1, 1)
    rough = jax.random.uniform(jax.random.fold_in(key, 505), (HEADS,), jnp.float32, 0.7, 1.4)
    return jnp.exp(position * jnp.log(ratio)) * rough


def draw_grad_out(key, part):
    shape = (LAYERS, TOKENS, HEADS, VDIM)
    ramp = 0.03 * head_ramp(key, 10.0)
    base = jnp.clip(jax.random.normal(jax.random.fold_in(key, 606), shape, jnp.float32), -3.0, 3.0)
    values = jnp.clip(base * ramp[None, None, :, None], -2.0, 2.0)
    return values.reshape(LAYERS, TOKENS, HEADS * VDIM).astype(jnp.bfloat16)


def draw_momentum(key, part):
    shape = (LAYERS, LATENT, HEADS, NOPE + VDIM)
    ramp = 0.2 * head_ramp(key, 10.0)
    base = jnp.clip(jax.random.normal(jax.random.fold_in(key, 707), shape, jnp.float32), -3.0, 3.0)
    values = jnp.clip(base * ramp[None, None, :, None], -16.0, 16.0)
    return values.reshape(LAYERS, LATENT, HEADS * (NOPE + VDIM)).astype(jnp.bfloat16)


def block_levels(key, dims, shards, smallest, largest):
    def one(dim, parts):
        heights = jax.random.uniform(jax.random.fold_in(jax.random.fold_in(key, 6), dim), (parts,), jnp.float32, smallest / len(shards), largest / len(shards))
        return jnp.repeat(jnp.exp(heights), dims[dim] // parts).reshape((-1,) + (1,) * (len(dims) - dim - 1))

    factor_of = one(*shards[0])
    for cut in shards[1:]:
        factor_of = factor_of * one(*cut)
    return factor_of


def scatter_about(rng, extent, deviation, bound, pieces=(), kind=jnp.bfloat16):
    array = deviation * jax.random.normal(rng, extent, jnp.float32)
    if pieces:
        array = array * block_levels(rng, extent, pieces, -0.22, 0.18)
    return jnp.clip(array, -bound, bound).astype(kind)


def setup_inputs(seed: int = 0) -> dict:
    key_of = jax.random.split(jax.random.key(seed), 7)
    return {
        "latent": scatter_about(key_of[0], (LAYERS, TOKENS, LATENT), 1.0, 6.0, ((1, 8),)),
        "rope_keys": draw_rope_keys(jax.random.fold_in(key_of[6], 71), 0),
        "queries": draw_queries(jax.random.fold_in(key_of[6], 71), 0),
        "grad_out": draw_grad_out(jax.random.fold_in(key_of[6], 71), 0),
        "key_value_up_weight": scatter_about(key_of[4], (LAYERS, LATENT, COLS), LATENT ** -0.5, 0.25, ((0, 8), (2, 32))),
        "momentum": draw_momentum(jax.random.fold_in(key_of[6], 71), 0),
    }


poly_first = 3.4445
poly_second = -4.775
poly_third = 2.0315
norm_epsilon = 1e-07
decay_rate = 0.95

def sequence_grads(compressed_latent_rows, rotary_position_rows, query_rows, grad_rows, weight_cols):
    rows = compressed_latent_rows.shape[0]
    score_scale = 1.0 / math.sqrt(NOPE + ROPE)
    kv_rows = jnp.dot(compressed_latent_rows, weight_cols, preferred_element_type=jnp.float32).astype(jnp.bfloat16)
    kv_rows = kv_rows.reshape(rows, HEADS, NOPE + VDIM).astype(jnp.float32)
    key_nope = kv_rows[:, :, :NOPE]
    values = kv_rows[:, :, NOPE:]
    query_all = query_rows.reshape(rows, HEADS, NOPE + ROPE).astype(jnp.float32)
    query_nope = query_all[:, :, :NOPE]
    query_rope = query_all[:, :, NOPE:]
    scores = jnp.einsum('shd,thd->hst', query_nope, key_nope)
    scores = scores + jnp.einsum('shd,td->hst', query_rope, rotary_position_rows.astype(jnp.float32))
    scores = scores * score_scale
    places = jnp.arange(rows)
    allowed = places[None, :] <= places[:, None]
    scores = jnp.where(allowed[None], scores, -jnp.inf)
    top_score = lax.optimization_barrier(jnp.max(scores, axis=-1, keepdims=True))
    expd = jnp.exp(scores - top_score)
    probs = expd / lax.optimization_barrier(jnp.sum(expd, axis=-1, keepdims=True))
    probs_low = probs.astype(jnp.bfloat16).astype(jnp.float32)
    grad_heads = grad_rows.reshape(rows, HEADS, VDIM).astype(jnp.float32)
    grad_values = jnp.einsum('hst,shd->thd', probs_low, grad_heads)
    grad_probs = jnp.einsum('shd,thd->hst', grad_heads, values)
    row_delta = lax.optimization_barrier(jnp.sum(probs * grad_probs, axis=-1, keepdims=True))
    grad_scores = (probs * (grad_probs - row_delta) * score_scale).astype(jnp.bfloat16).astype(jnp.float32)
    grad_keys = jnp.einsum('hst,shd->thd', grad_scores, query_nope)
    joined = jnp.concatenate([grad_keys, grad_values], axis=-1).astype(jnp.bfloat16)
    return joined.reshape(rows, HEADS * (NOPE + VDIM))

def orthogonal(source):
    highest = lax.Precision.HIGHEST
    norm_value = jnp.sqrt(jnp.sum(source * source)) + norm_epsilon
    base = jnp.dot(source, source.T, precision=highest) / (norm_value * norm_value)
    identity_matrix = jnp.eye(source.shape[0], dtype=jnp.float32)
    mixer = identity_matrix
    for count_index in range(STEPS):
        inner = jnp.dot(jnp.dot(mixer, base, precision=highest), mixer.T, precision=highest)
        poly = poly_first * identity_matrix + poly_second * inner + poly_third * jnp.dot(inner, inner, precision=highest)
        mixer = jnp.dot(poly, mixer, precision=highest)
    return jnp.dot(mixer, source, precision=highest) / norm_value

def reference(latent, rope_keys, queries, grad_out, key_value_up_weight, momentum):
    update_scale = 0.2 * math.sqrt(max(LATENT, COLS))
    momenta = []
    updates = []
    for layer_index in range(LAYERS):
        total = jnp.zeros((LATENT, COLS), jnp.float32)
        for group_index in range(N_DP):
            low = group_index * SEQ
            compressed_latent_rows = latent[layer_index, low:low + SEQ]
            dkv = sequence_grads(compressed_latent_rows, rope_keys[layer_index, low:low + SEQ], queries[layer_index, low:low + SEQ], grad_out[layer_index, low:low + SEQ], key_value_up_weight[layer_index])
            partial_value = jnp.dot(compressed_latent_rows.T, dkv, preferred_element_type=jnp.float32).astype(jnp.bfloat16)
            partial_value = lax.optimization_barrier(partial_value)
            total = total + partial_value.astype(jnp.float32)
        fresh = (decay_rate * momentum[layer_index].astype(jnp.float32) + total).astype(jnp.bfloat16)
        momenta.append(fresh)
        updates.append(update_scale * orthogonal(fresh.astype(jnp.float32)))
    return (jnp.stack(momenta), jnp.stack(updates))
```

```python
import math

import jax
import jax.numpy as jnp
from jax import lax
from jax.experimental import pallas as pl
from jax.experimental.pallas import tpu as pltpu
from jax.sharding import Mesh
from jax.sharding import PartitionSpec as P

LATENT = 512
HEADS = 128
NOPE = 128
ROPE = 64
VDIM = 128
SEQ = 128
HD = 4
QW = NOPE + ROPE
KVW = NOPE + VDIM
COLS_HERE = HD * KVW
WIDE = HD * QW + HD * VDIM
TILE = 128
NT = LATENT // TILE
PAIRS = [(a, b) for a in range(NT) for b in range(a, NT)]

DP = ("zl", "core")
YX = ("y", "x")
NDP = 8
NYX = 16
ROWS = SEQ // NYX

poly_first = 3.4445
poly_second = -4.775
poly_third = 2.0315
norm_epsilon = 1e-07
decay_rate = 0.95

F32 = jnp.float32
BF16 = jnp.bfloat16
GROUPS = ((0, 1), (2, 3), (4, 5), (6, 7))


def contract_last(a, b):
    return lax.dot_general(a, b, (((1,), (1,)), ((), ())), preferred_element_type=F32)


def attend(rows, tokens, weight):
    scale = 1.0 / math.sqrt(QW)
    kv = jnp.dot(rows[:, :LATENT], weight, preferred_element_type=F32).astype(BF16)
    rope = rows[:, LATENT:]
    key_at = lax.broadcasted_iota(jnp.int32, (SEQ, SEQ), 0)
    query_at = lax.broadcasted_iota(jnp.int32, (SEQ, SEQ), 1)
    allowed = key_at <= query_at
    out = []
    for h in range(HD):
        keys = kv[:, h * KVW : h * KVW + NOPE]
        values = kv[:, h * KVW + NOPE : (h + 1) * KVW]
        query = tokens[:, h * QW : (h + 1) * QW]
        cot = tokens[:, HD * QW + h * VDIM : HD * QW + (h + 1) * VDIM]
        scores = contract_last(jnp.concatenate([keys, rope], axis=1), query) * scale
        scores = jnp.where(allowed, scores, -jnp.inf)
        expd = jnp.exp(scores - jnp.max(scores, axis=0, keepdims=True))
        probs = expd * (1.0 / jnp.sum(expd, axis=0, keepdims=True))
        grad_values = jnp.dot(probs.astype(BF16), cot, preferred_element_type=F32)
        grad_probs = contract_last(values, cot)
        delta = jnp.sum(probs * grad_probs, axis=0, keepdims=True)
        grad_scores = (probs * (grad_probs - delta) * scale).astype(BF16)
        grad_keys = jnp.dot(grad_scores, query[:, :NOPE], preferred_element_type=F32)
        out += [grad_keys.astype(BF16), grad_values.astype(BF16)]
    return jnp.concatenate(out, axis=1)


def attention(rows, weight, chunks, first):
    n = len(chunks)

    def kernel(rows_ref, weight_ref, *refs):
        for k in range(n):
            refs[n][k * SEQ : (k + 1) * SEQ, :] = attend(rows_ref[k], refs[k][...], weight_ref[...])

    whole = lambda shape: pl.BlockSpec(shape, lambda t: (0,) * len(shape))
    return pl.pallas_call(
        kernel,
        grid=(1,),
        in_specs=[
            pl.BlockSpec((n, SEQ, LATENT + ROPE), lambda t: (first // n, 0, 0)),
            whole((LATENT, COLS_HERE)),
        ]
        + [whole((SEQ, WIDE))] * n,
        out_specs=whole((n * SEQ, COLS_HERE)),
        out_shape=jax.ShapeDtypeStruct((n * SEQ, COLS_HERE), BF16),
        name=f"attention_{first}",
    )(rows, weight, *chunks)


def momentum_and_gram(latent_t, parts, momentum):
    n = len(parts)
    width = KVW

    def kernel(lat_ref, mom_ref, *refs):
        fresh_ref, gram_ref, acc_ref = refs[n], refs[n + 1], refs[n + 2]
        step = pl.program_id(0)
        total = decay_rate * mom_ref[...].astype(F32)
        at = 0
        for k in range(n):
            rows = parts[k].shape[0]
            total = total + jnp.dot(lat_ref[:, at : at + rows], refs[k][...], preferred_element_type=F32)
            at += rows
        fresh = total.astype(BF16)
        fresh_ref[...] = fresh
        half = LATENT // 2
        top = contract_last(fresh[:half], fresh)
        low = contract_last(fresh[half:], fresh[half:])

        @pl.when(step == 0)
        def _():
            acc_ref[:half, :] = top
            acc_ref[half:, half:] = low

        @pl.when(step > 0)
        def _():
            acc_ref[:half, :] += top
            acc_ref[half:, half:] += low

        @pl.when(step == pl.num_programs(0) - 1)
        def _():
            for k, (a, b) in enumerate(PAIRS):
                gram_ref[k] = acc_ref[a * TILE : (a + 1) * TILE, b * TILE : (b + 1) * TILE].astype(BF16)

    return pl.pallas_call(
        kernel,
        grid=(COLS_HERE // width,),
        in_specs=[
            pl.BlockSpec((LATENT, NDP * SEQ), lambda t: (0, 0)),
            pl.BlockSpec((LATENT, width), lambda t: (0, t)),
        ]
        + [pl.BlockSpec((p.shape[0], width), lambda t: (0, t)) for p in parts],
        out_specs=(
            pl.BlockSpec((LATENT, width), lambda t: (0, t)),
            pl.BlockSpec((len(PAIRS), TILE, TILE), lambda t: (0, 0, 0)),
        ),
        out_shape=(
            jax.ShapeDtypeStruct((LATENT, COLS_HERE), BF16),
            jax.ShapeDtypeStruct((len(PAIRS), TILE, TILE), BF16),
        ),
        scratch_shapes=[pltpu.VMEM((LATENT, LATENT), F32)],
        name="momentum_gram",
    )(latent_t, momentum, *parts)


def split(a):
    high = a.astype(BF16)
    return high, (a - high.astype(F32)).astype(BF16)


def product(a, b):
    d = lambda u, v: jnp.dot(u, v, preferred_element_type=F32)
    return d(a[0], b[0]) + (d(a[0], b[1]) + d(a[1], b[0]))


def update(gram, fresh):
    width = KVW
    update_scale = 0.2 * math.sqrt(max(LATENT, HEADS * KVW))

    def kernel(gram_ref, fresh_ref, out_ref, base_ref, high_ref, low_ref, factor_ref):
        @pl.when(pl.program_id(0) == 0)
        def _():
            row = lax.broadcasted_iota(jnp.int32, (TILE, TILE), 0)
            col = lax.broadcasted_iota(jnp.int32, (TILE, TILE), 1)
            on_diagonal = row == col
            squares = jnp.zeros((TILE, TILE), F32)
            for k, (a, b) in enumerate(PAIRS):
                block = gram_ref[k].astype(F32)
                if a == b:
                    squares = squares + jnp.where(on_diagonal, block, 0.0)
                base_ref[a * TILE : (a + 1) * TILE, b * TILE : (b + 1) * TILE] = block
                if a != b:
                    base_ref[b * TILE : (b + 1) * TILE, a * TILE : (a + 1) * TILE] = block.T
            squares = jnp.sum(jnp.sum(squares, axis=0, keepdims=True), axis=1, keepdims=True)
            norm = jnp.sqrt(squares) + norm_epsilon
            factor_ref[...] = jnp.broadcast_to(update_scale / norm, factor_ref.shape)
            wide_row = lax.broadcasted_iota(jnp.int32, (LATENT, LATENT), 0)
            wide_col = lax.broadcasted_iota(jnp.int32, (LATENT, LATENT), 1)
            first = jnp.where(wide_row == wide_col, poly_first, 0.0).astype(F32)
            base = base_ref[...] * (1.0 / (norm * norm))
            base2 = split(base)
            poly = first + poly_second * base + poly_third * product(base2, base2)
            poly2 = split(poly)
            inner = product(base2, split(product(poly2, poly2)))
            inner2 = split(inner)
            later = first + poly_second * inner + poly_third * product(inner2, inner2)
            high, low = split(product(split(later), poly2))
            high_ref[...] = high
            low_ref[...] = low

        fresh = fresh_ref[...]
        mixed = jnp.dot(high_ref[...], fresh, preferred_element_type=F32) + jnp.dot(
            low_ref[...], fresh, preferred_element_type=F32
        )
        out_ref[...] = mixed * factor_ref[0:1, 0:1]

    return pl.pallas_call(
        kernel,
        grid=(COLS_HERE // width,),
        in_specs=[
            pl.BlockSpec((len(PAIRS), TILE, TILE), lambda t: (0, 0, 0)),
            pl.BlockSpec((LATENT, width), lambda t: (0, t)),
        ],
        out_specs=pl.BlockSpec((LATENT, width), lambda t: (0, t)),
        out_shape=jax.ShapeDtypeStruct((LATENT, COLS_HERE), F32),
        scratch_shapes=[
            pltpu.VMEM((LATENT, LATENT), F32),
            pltpu.VMEM((LATENT, LATENT), BF16),
            pltpu.VMEM((LATENT, LATENT), BF16),
            pltpu.VMEM((8, TILE), F32),
        ],
        name="update",
    )(gram, fresh)


def reduce_gram(gram):
    pieces = gram.reshape(NYX, -1, TILE)
    got = lax.all_to_all(pieces, YX, 0, 0, tiled=True)
    mine = jnp.sum(got.astype(F32), axis=0).astype(BF16)
    other = lax.ppermute(mine, "zh", [(0, 1), (1, 0)])
    mine = (mine.astype(F32) + other.astype(F32)).astype(BF16)
    full = lax.all_to_all(jnp.broadcast_to(mine[None], pieces.shape), YX, 0, 0, tiled=True)
    return full.reshape(gram.shape)


def pick(a, index):
    return lax.dynamic_index_in_dim(a, index, 0, keepdims=False)


def body(latent, rope_keys, queries, grad_out, key_value_up_weight, momentum):
    here = lax.axis_index(DP)
    chunks = []
    for s in range(NDP):
        chunk = jnp.concatenate([pick(queries, here ^ s), pick(grad_out, here ^ s)], axis=1)
        if s:
            chunk = lax.ppermute(chunk, DP, [(k, k ^ s) for k in range(NDP)])
        chunks.append(chunk)
    rows = jnp.concatenate([latent, rope_keys], axis=2)
    rows = lax.dynamic_slice_in_dim(rows, ROWS * lax.axis_index(YX), ROWS, axis=1)
    rows = lax.all_to_all(rows, DP, 0, 0, tiled=True)
    rows = jnp.stack([pick(rows, here ^ s) for s in range(NDP)])
    rows = lax.all_to_all(jnp.broadcast_to(rows[None], (NYX,) + rows.shape), YX, 0, 0, tiled=True)
    rows = rows.transpose(1, 0, 2, 3).reshape(NDP, SEQ, LATENT + ROPE)
    latent_t = rows.reshape(NDP * SEQ, LATENT + ROPE)[:, :LATENT].T

    weight = key_value_up_weight[0]
    parts = [attention(rows, weight, [chunks[s] for s in group], group[0]) for group in GROUPS]
    fresh, gram = momentum_and_gram(latent_t, parts, momentum[0])
    step = update(reduce_gram(gram), fresh)
    return fresh[None], step[None]


def solution(mesh):
    fine = Mesh(mesh.devices.reshape(4, 2, 4, 4, 2), ("zl", "core", "y", "x", "zh"))
    heads = ("y", "x", "zh")
    placed = (
        P(None, DP, None),
        P(None, DP, None),
        P(None, DP, heads),
        P(None, DP, heads),
        P(DP, None, heads),
        P(DP, None, heads),
    )
    return jax.shard_map(
        body,
        mesh=fine,
        in_specs=placed,
        out_specs=(P(DP, None, heads), P(DP, None, heads)),
        check_vma=False,
    )
```

```python
import math

import jax
import jax.numpy as jnp
from jax import lax
from jax.experimental import pallas as pl
from jax.experimental.pallas import tpu as pltpu
from jax.sharding import Mesh
from jax.sharding import PartitionSpec as P


LATENT = 512
HEADS = 128
NOPE = 128
ROPE = 64
VDIM = 128
SEQ = 128
HD = 4
QW = NOPE + ROPE
KVW = NOPE + VDIM
COLS_HERE = HD * KVW
TILE = 128
NT = LATENT // TILE
PAIRS = [(a, b) for a in range(NT) for b in range(a, NT)]

DP = ("zl", "core")
YX = ("y", "x")
NDP = 8
NYX = 16
ROWS = SEQ // NYX

poly_first = 3.4445
poly_second = -4.775
poly_third = 2.0315
norm_epsilon = 1e-07
decay_rate = 0.95

F32 = jnp.float32
BF16 = jnp.bfloat16


def contract_last(a, b):
    return lax.dot_general(a, b, (((1,), (1,)), ((), ())), preferred_element_type=F32)


def contract_first(a, b):
    return lax.dot_general(a, b, (((0,), (0,)), ((), ())), preferred_element_type=F32)


def up_project(rows, weight):
    return jnp.dot(rows[:, :LATENT], weight, preferred_element_type=F32).astype(BF16)


def attend(rows, kv, tokens):
    scale = 1.0 / math.sqrt(QW)
    key_at = lax.broadcasted_iota(jnp.int32, (SEQ, SEQ), 0)
    query_at = lax.broadcasted_iota(jnp.int32, (SEQ, SEQ), 1)
    allowed = key_at <= query_at
    queries, cots, scores, grad_probs = [], [], [], []
    for k in range(len(tokens)):
        at = slice(k * SEQ, (k + 1) * SEQ)
        for h in range(HD):
            keys = kv[at, h * KVW : h * KVW + NOPE]
            values = kv[at, h * KVW + NOPE : (h + 1) * KVW]
            query = tokens[k][:, h * QW : (h + 1) * QW]
            cot = tokens[k][:, HD * QW + h * VDIM : HD * QW + (h + 1) * VDIM]
            queries.append(query[:, :NOPE])
            cots.append(cot)
            scores.append(contract_last(jnp.concatenate([keys, rows[at, LATENT:]], axis=1), query))
            grad_probs.append(contract_last(values, cot))
    low, grads = [], []
    for score, grad_prob in zip(scores, grad_probs):
        score = jnp.where(allowed, score * scale, -jnp.inf)
        expd = jnp.exp(score - jnp.max(score, axis=0, keepdims=True))
        probs = expd * (1.0 / jnp.sum(expd, axis=0, keepdims=True))
        delta = jnp.sum(probs * grad_prob, axis=0, keepdims=True)
        low.append(probs.astype(BF16))
        grads.append((probs * (grad_prob - delta) * scale).astype(BF16))
    out = []
    for query, cot, probs, grad in zip(queries, cots, low, grads):
        out.append(jnp.dot(grad, query, preferred_element_type=F32).astype(BF16))
        out.append(jnp.dot(probs, cot, preferred_element_type=F32).astype(BF16))
    wide = 2 * HD
    return jnp.concatenate([jnp.concatenate(out[k * wide : (k + 1) * wide], axis=1) for k in range(len(tokens))], axis=0)


IN_VMEM = pl.BlockSpec(memory_space=pltpu.VMEM)


def read_chunks(chunks, refs):
    out, at = [], 0
    for parts in chunks:
        got = [r[...] for r in refs[at : at + len(parts)]]
        at += len(parts)
        if len(parts) == 2:
            half = HD * QW // 2
            got = [jnp.concatenate([g[:, :half] for g in got] + [g[:, half:] for g in got], axis=1)]
        out.append(got[0])
    return out


def first_sequences(rows, weight, chunks):
    n = len(chunks)
    flat = [part for parts in chunks for part in parts]

    def kernel(rows_ref, weight_ref, *refs):
        here = rows_ref[:n].reshape(n * SEQ, LATENT + ROPE)
        refs[-1][...] = attend(here, up_project(here, weight_ref[...]), read_chunks(chunks, refs))

    return pl.pallas_call(
        kernel,
        in_specs=[IN_VMEM] * (2 + len(flat)),
        out_specs=IN_VMEM,
        out_shape=jax.ShapeDtypeStruct((n * SEQ, COLS_HERE), BF16),
        name="first_sequences",
    )(rows, weight, *flat)


def middle_sequences(rows, weight, before, momentum, chunks):
    first, n = before.shape[0] // SEQ, len(chunks)
    flat = [part for parts in chunks for part in parts]

    def kernel(rows_ref, weight_ref, before_ref, mom_ref, *refs):
        sofar_ref, kv_ref = refs[-2], refs[-1]
        here = rows_ref[first:].reshape((n + 1) * SEQ, LATENT + ROPE)
        kv = up_project(here, weight_ref[...])
        kv_ref[...] = kv[n * SEQ :]
        dkv = jnp.concatenate([before_ref[...], attend(here, kv, read_chunks(chunks, refs))], axis=0)
        lat = rows_ref[: first + n].reshape((first + n) * SEQ, LATENT + ROPE)[:, :LATENT]
        sofar_ref[...] = decay_rate * mom_ref[...].astype(F32) + contract_first(lat, dkv)

    return pl.pallas_call(
        kernel,
        in_specs=[IN_VMEM] * (4 + len(flat)),
        out_specs=(IN_VMEM, IN_VMEM),
        out_shape=(
            jax.ShapeDtypeStruct((LATENT, COLS_HERE), F32),
            jax.ShapeDtypeStruct((SEQ, COLS_HERE), BF16),
        ),
        name="middle_sequences",
    )(rows, weight, before, momentum, *flat)


def last_sequence(rows, kv, sofar, chunk):
    half = LATENT // 2
    split_at = NT // 2

    def kernel(rows_hbm, kv_ref, chunk_ref, sofar_hbm, fresh_ref, gram_ref, rows_ref, sofar_ref, sems):
        load = pltpu.make_async_copy(sofar_hbm, sofar_ref, sems.at[0])
        load.start()
        load_rows = pltpu.make_async_copy(rows_hbm.at[NDP - 1], rows_ref, sems.at[1])
        load_rows.start()
        load_rows.wait()
        rows = rows_ref[...]
        dkv = attend(rows, kv_ref[...], [chunk_ref[...]])
        add = contract_first(rows[:, :LATENT], dkv)
        load.wait()
        fresh = (sofar_ref[...] + add).astype(BF16)
        fresh_ref[...] = fresh
        top = contract_last(fresh[:half], fresh).astype(BF16)
        low = contract_last(fresh[half:], fresh[half:]).astype(BF16)
        for k, (a, b) in enumerate(PAIRS):
            if a < split_at:
                gram_ref[k] = top[a * TILE : (a + 1) * TILE, b * TILE : (b + 1) * TILE]
            else:
                a, b = a - split_at, b - split_at
                gram_ref[k] = low[a * TILE : (a + 1) * TILE, b * TILE : (b + 1) * TILE]

    return pl.pallas_call(
        kernel,
        in_specs=[pl.BlockSpec(memory_space=pl.ANY), IN_VMEM, IN_VMEM, pl.BlockSpec(memory_space=pl.ANY)],
        out_specs=(IN_VMEM, IN_VMEM),
        out_shape=(
            jax.ShapeDtypeStruct((LATENT, COLS_HERE), BF16),
            jax.ShapeDtypeStruct((len(PAIRS), TILE, TILE), BF16),
        ),
        scratch_shapes=[
            pltpu.VMEM((SEQ, LATENT + ROPE), BF16),
            pltpu.VMEM((LATENT, COLS_HERE), F32),
            pltpu.SemaphoreType.DMA((2,)),
        ],
        name="last_sequence",
    )(rows, kv, chunk, sofar)


def split(a):
    high = a.astype(BF16)
    return high, (a - high.astype(F32)).astype(BF16)


def product(a, b):
    d = lambda u, v: jnp.dot(u, v, preferred_element_type=F32)
    return d(a[0], b[0]) + (d(a[0], b[1]) + d(a[1], b[0]))


def to_unit(t):
    p = jnp.ones_like(t)
    for e in (64, 32, 16, 8, 4, 2, 1):
        big = t >= 2.0**e
        t = jnp.where(big, t * 2.0**-e, t)
        p = jnp.where(big, p * 2.0**-e, p)
    for e in (64, 32, 16, 8, 4, 2, 1):
        small = t < 2.0 ** (1 - e)
        t = jnp.where(small, t * 2.0**e, t)
        p = jnp.where(small, p * 2.0**e, p)
    return t, p


def dot(a, b):
    return jnp.dot(a, b, preferred_element_type=F32)


def update(gram, fresh):
    width = COLS_HERE // 2
    update_scale = 0.2 * math.sqrt(max(LATENT, HEADS * KVW))

    def kernel(gram_ref, fresh_ref, out_ref, base_ref, high_ref, low_ref, factor_ref):
        @pl.when(pl.program_id(0) == 0)
        def _():
            on_diagonal = lax.broadcasted_iota(jnp.int32, (TILE, TILE), 0) == lax.broadcasted_iota(
                jnp.int32, (TILE, TILE), 1
            )
            squares = jnp.zeros((TILE, TILE), F32)
            for k, (a, b) in enumerate(PAIRS):
                if a == b:
                    squares = squares + jnp.where(on_diagonal, gram_ref[k].astype(F32), 0.0)
            squares = jnp.sum(jnp.sum(squares, axis=0, keepdims=True), axis=1, keepdims=True)
            norm = jnp.sqrt(squares) + norm_epsilon
            factor_ref[...] = jnp.broadcast_to(update_scale / norm, factor_ref.shape)
            ratio, power = to_unit(norm * norm)
            for k, (a, b) in enumerate(PAIRS):
                block = gram_ref[k].astype(F32) * power
                base_ref[a * TILE : (a + 1) * TILE, b * TILE : (b + 1) * TILE] = block.astype(BF16)
                if a != b:
                    base_ref[b * TILE : (b + 1) * TILE, a * TILE : (a + 1) * TILE] = block.T.astype(BF16)
            inv = 1.0 / ratio
            first = jnp.where(
                lax.broadcasted_iota(jnp.int32, (LATENT, LATENT), 0)
                == lax.broadcasted_iota(jnp.int32, (LATENT, LATENT), 1),
                poly_first,
                0.0,
            ).astype(F32)
            base = base_ref[...]
            poly = split(first + (poly_second * inv) * base.astype(F32) + (poly_third * inv * inv) * dot(base, base))
            square = split(product(poly, poly))
            inner = inv * (dot(base, square[0]) + dot(base, square[1]))
            inner2 = split(inner)
            later = first + poly_second * inner + poly_third * product(inner2, inner2)
            high, low = split(product(split(later), poly))
            high_ref[...] = high
            low_ref[...] = low

        fresh = fresh_ref[...]
        out_ref[...] = (dot(high_ref[...], fresh) + dot(low_ref[...], fresh)) * factor_ref[0:1, 0:1]

    return pl.pallas_call(
        kernel,
        grid=(COLS_HERE // width,),
        in_specs=[
            pl.BlockSpec((len(PAIRS), TILE, TILE), lambda t: (0, 0, 0)),
            pl.BlockSpec((LATENT, width), lambda t: (0, t)),
        ],
        out_specs=pl.BlockSpec((LATENT, width), lambda t: (0, t)),
        out_shape=jax.ShapeDtypeStruct((LATENT, COLS_HERE), F32),
        scratch_shapes=[
            pltpu.VMEM((LATENT, LATENT), BF16),
            pltpu.VMEM((LATENT, LATENT), BF16),
            pltpu.VMEM((LATENT, LATENT), BF16),
            pltpu.VMEM((8, TILE), F32),
        ],
        name="update",
    )(gram, fresh)


def reduce_gram(gram):
    pieces = gram.reshape(NYX, -1, TILE)
    got = lax.all_to_all(pieces, YX, 0, 0, tiled=True)
    mine = jnp.sum(got.astype(F32), axis=0).astype(BF16)
    other = lax.ppermute(mine, "zh", [(0, 1), (1, 0)])
    mine = (mine.astype(F32) + other.astype(F32)).astype(BF16)
    full = lax.all_to_all(jnp.broadcast_to(mine[None], pieces.shape), YX, 0, 0, tiled=True)
    return full.reshape(gram.shape)


def pick(a, index):
    return lax.dynamic_index_in_dim(a, index, 0, keepdims=False)


STEPS_FIRST = (0, 6, 7, 2)
STEPS_MIDDLE = (1, 3, 4)
STEP_LAST = 5
STEP_OPENING = 6
ORDER = STEPS_FIRST + STEPS_MIDDLE + (STEP_LAST,)
HALF_Q = HD * QW // 2
HALF_V = HD * VDIM // 2


def pack(queries, grad_out, cuts):
    widths = [(q.stop - q.start, v.stop - v.start) for _, q, v in cuts]

    def kernel(queries_ref, grads_ref, *refs):
        n = len(cuts)
        here = lax.axis_index(DP)
        copies = []
        for k, (s, q, v) in enumerate(cuts):
            wide = widths[k][0]
            copies.append(
                pltpu.make_async_copy(
                    queries_ref.at[here ^ s, :, q], refs[k].at[:, :wide], refs[n].at[2 * k]
                )
            )
            copies.append(
                pltpu.make_async_copy(
                    grads_ref.at[here ^ s, :, v], refs[k].at[:, wide:], refs[n].at[2 * k + 1]
                )
            )
        for copy in copies:
            copy.start()
        for copy in copies:
            copy.wait()

    anywhere = pl.BlockSpec(memory_space=pl.ANY)
    return pl.pallas_call(
        kernel,
        in_specs=[anywhere, anywhere],
        out_specs=[IN_VMEM] * len(cuts),
        out_shape=[jax.ShapeDtypeStruct((SEQ, a + b), BF16) for a, b in widths],
        scratch_shapes=[pltpu.SemaphoreType.DMA((2 * len(cuts),))],
    )(queries, grad_out)


def send(chunk, s):
    return lax.ppermute(chunk, DP, [(k, k ^ s) for k in range(NDP)])


def inner_body(latent, rope_keys, queries, grad_out, key_value_up_weight, momentum):
    here = lax.axis_index(DP)
    halves = pack(
        queries,
        grad_out,
        [(STEP_OPENING, slice(k * HALF_Q, (k + 1) * HALF_Q), slice(k * HALF_V, (k + 1) * HALF_V)) for k in range(2)],
    )
    halves, queries, grad_out, latent, rope_keys = lax.optimization_barrier(
        (halves, queries, grad_out, latent, rope_keys)
    )
    others = [s for s in ORDER if s != STEP_OPENING]
    packed = pack(queries, grad_out, [(s, slice(0, HD * QW), slice(0, HD * VDIM)) for s in others])
    chunks = {s: (send(chunk, s) if s else chunk,) for s, chunk in zip(others, packed)}
    chunks[STEP_OPENING] = tuple(send(h, STEP_OPENING) for h in halves)
    at = ROWS * lax.axis_index(YX)
    rows = jnp.concatenate(
        [lax.dynamic_slice_in_dim(latent, at, ROWS, axis=1), lax.dynamic_slice_in_dim(rope_keys, at, ROWS, axis=1)],
        axis=2,
    )
    rows = lax.all_to_all(rows, DP, 0, 0, tiled=True)
    rows = jnp.stack([pick(rows, here ^ s) for s in ORDER])
    rows = lax.all_to_all(jnp.broadcast_to(rows[None], (NYX,) + rows.shape), YX, 0, 0, tiled=True)
    rows = rows.transpose(1, 0, 2, 3).reshape(NDP, SEQ, LATENT + ROPE)

    weight = key_value_up_weight[0]
    dkv = first_sequences(rows, weight, [chunks[s] for s in STEPS_FIRST])
    sofar, kv = middle_sequences(rows, weight, dkv, momentum[0], [chunks[s] for s in STEPS_MIDDLE])
    fresh, gram = last_sequence(rows, kv, sofar, chunks[STEP_LAST][0])
    step = update(reduce_gram(gram), fresh)
    return fresh[None], step[None]


def solution(mesh):
    fine = Mesh(mesh.devices.reshape(4, 2, 4, 4, 2), ("zl", "core", "y", "x", "zh"))
    heads = ("y", "x", "zh")
    placed = (
        P(None, DP, None),
        P(None, DP, None),
        P(None, DP, heads),
        P(None, DP, heads),
        P(DP, None, heads),
        P(DP, None, heads),
    )
    return jax.shard_map(
        inner_body,
        mesh=fine,
        in_specs=placed,
        out_specs=(P(DP, None, heads), P(DP, None, heads)),
        check_vma=False,
    )
```

```python
import math

import jax
import jax.numpy as jnp
from jax import lax
from jax.experimental import pallas as pl
from jax.experimental.pallas import tpu as pltpu
from jax.sharding import Mesh
from jax.sharding import PartitionSpec as P


LATENT = 512
HEADS = 128
NOPE = 128
ROPE = 64
VDIM = 128
SEQ = 128
HD = 4
QW = NOPE + ROPE
KVW = NOPE + VDIM
COLS_HERE = HD * KVW
TILE = 128
NT = LATENT // TILE
PAIRS = [(a, b) for a in range(NT) for b in range(a, NT)]

DP = ("zl", "core")
YX = ("y", "x")
NDP = 8
NYX = 16
ROWS = SEQ // NYX

poly_first = 3.4445
poly_second = -4.775
poly_third = 2.0315
norm_epsilon = 1e-07
decay_rate = 0.95

F32 = jnp.float32
BF16 = jnp.bfloat16
VMEM_LIMIT = 65000 * 1024


def contract_last(a, b):
    return lax.dot_general(a, b, (((1,), (1,)), ((), ())), preferred_element_type=F32)


def contract_first(a, b):
    return lax.dot_general(a, b, (((0,), (0,)), ((), ())), preferred_element_type=F32)


def up_project(rows, weight):
    return jnp.dot(rows[:, :LATENT], weight, preferred_element_type=F32).astype(BF16)


def attend(rows, kv, tokens):
    scale = 1.0 / math.sqrt(QW)
    key_at = lax.broadcasted_iota(jnp.int32, (SEQ, SEQ), 0)
    query_at = lax.broadcasted_iota(jnp.int32, (SEQ, SEQ), 1)
    allowed = key_at <= query_at
    queries, cots, scores, grad_probs = [], [], [], []
    for k in range(len(tokens)):
        at = slice(k * SEQ, (k + 1) * SEQ)
        for h in range(HD):
            keys = kv[at, h * KVW : h * KVW + NOPE]
            values = kv[at, h * KVW + NOPE : (h + 1) * KVW]
            query = tokens[k][:, h * QW : (h + 1) * QW]
            cot = tokens[k][:, HD * QW + h * VDIM : HD * QW + (h + 1) * VDIM]
            queries.append(query[:, :NOPE])
            cots.append(cot)
            scores.append(contract_last(jnp.concatenate([keys, rows[at, LATENT:]], axis=1), query))
            grad_probs.append(contract_last(values, cot))
    low, grads = [], []
    for score, grad_prob in zip(scores, grad_probs):
        score = jnp.where(allowed, score * scale, -jnp.inf)
        expd = jnp.exp(score - jnp.max(score, axis=0, keepdims=True))
        probs = expd * (1.0 / jnp.sum(expd, axis=0, keepdims=True))
        delta = jnp.sum(probs * grad_prob, axis=0, keepdims=True)
        low.append(probs.astype(BF16))
        grads.append((probs * (grad_prob - delta) * scale).astype(BF16))
    out = []
    for query, cot, probs, grad in zip(queries, cots, low, grads):
        out.append(jnp.dot(grad, query, preferred_element_type=F32).astype(BF16))
        out.append(jnp.dot(probs, cot, preferred_element_type=F32).astype(BF16))
    wide = 2 * HD
    return jnp.concatenate([jnp.concatenate(out[k * wide : (k + 1) * wide], axis=1) for k in range(len(tokens))], axis=0)


IN_VMEM = pl.BlockSpec(memory_space=pltpu.VMEM)


def read_chunks(chunks, refs):
    out, at = [], 0
    for parts in chunks:
        got = [r[...] for r in refs[at : at + len(parts)]]
        at += len(parts)
        if len(parts) == 2:
            half = HD * QW // 2
            got = [jnp.concatenate([g[:, :half] for g in got] + [g[:, half:] for g in got], axis=1)]
        out.append(got[0])
    return out


ROOMY = pltpu.CompilerParams(vmem_limit_bytes=VMEM_LIMIT)


def first_sequences(rows, weight, momentum, chunks):
    n = len(chunks)
    flat = [part for parts in chunks for part in parts]

    def kernel(rows_ref, weight_ref, mom_ref, *refs):
        here = rows_ref[:n].reshape(n * SEQ, LATENT + ROPE)
        dkv = attend(here, up_project(here, weight_ref[...]), read_chunks(chunks, refs))
        refs[-1][...] = decay_rate * mom_ref[...].astype(F32) + contract_first(here[:, :LATENT], dkv)

    return pl.pallas_call(
        kernel,
        in_specs=[IN_VMEM] * (3 + len(flat)),
        out_specs=IN_VMEM,
        out_shape=jax.ShapeDtypeStruct((LATENT, COLS_HERE), F32),
        compiler_params=ROOMY,
        name="first_sequences",
    )(rows, weight, momentum, *flat)


def middle_sequences(rows, weight, sofar, first, chunks):
    n = len(chunks)
    flat = [part for parts in chunks for part in parts]

    def kernel(rows_ref, weight_ref, sofar_ref, *refs):
        out_ref, kv_ref, last_ref, turned_ref = refs[-4:]
        here = rows_ref[first:].reshape((n + 1) * SEQ, LATENT + ROPE)
        kv = up_project(here, weight_ref[...])
        kv_ref[...] = kv[n * SEQ :]
        last = here[n * SEQ :]
        last_ref[...] = last
        turned_ref[...] = last[:, :LATENT].T
        dkv = attend(here, kv, read_chunks(chunks, refs))
        out_ref[...] = sofar_ref[...] + contract_first(here[: n * SEQ, :LATENT], dkv)

    return pl.pallas_call(
        kernel,
        in_specs=[IN_VMEM] * (3 + len(flat)),
        out_specs=(IN_VMEM,) * 4,
        out_shape=(
            jax.ShapeDtypeStruct((LATENT, COLS_HERE), F32),
            jax.ShapeDtypeStruct((SEQ, COLS_HERE), BF16),
            jax.ShapeDtypeStruct((SEQ, LATENT + ROPE), BF16),
            jax.ShapeDtypeStruct((LATENT, SEQ), BF16),
        ),
        compiler_params=ROOMY,
        name="middle_sequences",
    )(rows, weight, sofar, *flat)


def last_sequence(rows, turned, kv, sofar, chunk):
    half = LATENT // 2
    split_at = NT // 2

    def kernel(rows_ref, turned_ref, kv_ref, chunk_ref, sofar_hbm, fresh_hbm, gram_ref, sofar_ref, fresh_ref, sems):
        load = pltpu.make_async_copy(sofar_hbm, sofar_ref, sems.at[0])
        load.start()
        dkv = attend(rows_ref[...], kv_ref[...], [chunk_ref[...]])
        add = dot(turned_ref[...], dkv)
        load.wait()
        fresh = (sofar_ref[...] + add).astype(BF16)
        fresh_ref[...] = fresh
        store = pltpu.make_async_copy(fresh_ref, fresh_hbm, sems.at[1])
        store.start()
        top = contract_last(fresh[:half], fresh).astype(BF16)
        low = contract_last(fresh[half:], fresh[half:]).astype(BF16)
        for k, (a, b) in enumerate(PAIRS):
            if a < split_at:
                gram_ref[k] = top[a * TILE : (a + 1) * TILE, b * TILE : (b + 1) * TILE]
            else:
                a, b = a - split_at, b - split_at
                gram_ref[k] = low[a * TILE : (a + 1) * TILE, b * TILE : (b + 1) * TILE]
        store.wait()

    anywhere = pl.BlockSpec(memory_space=pl.ANY)
    return pl.pallas_call(
        kernel,
        in_specs=[IN_VMEM] * 4 + [anywhere],
        out_specs=(anywhere, IN_VMEM),
        out_shape=(
            jax.ShapeDtypeStruct((LATENT, COLS_HERE), BF16),
            jax.ShapeDtypeStruct((len(PAIRS), TILE, TILE), BF16),
        ),
        scratch_shapes=[
            pltpu.VMEM((LATENT, COLS_HERE), F32),
            pltpu.VMEM((LATENT, COLS_HERE), BF16),
            pltpu.SemaphoreType.DMA((2,)),
        ],
        name="last_sequence",
    )(rows, turned, kv, chunk, sofar)


def split(a):
    high = a.astype(BF16)
    return high, (a - high.astype(F32)).astype(BF16)


def product(a, b):
    d = lambda u, v: jnp.dot(u, v, preferred_element_type=F32)
    return d(a[0], b[0]) + (d(a[0], b[1]) + d(a[1], b[0]))


def to_range(t):
    p = jnp.full_like(t, 2.0**64)
    for edge in (-48, -16, 16, 48, 80):
        p = jnp.where(t >= 2.0**edge, 2.0 ** -(edge + 16), p)
    return t * p, p


def dot(a, b):
    return jnp.dot(a, b, preferred_element_type=F32)


def update(gram, fresh):
    update_scale = 0.2 * math.sqrt(max(LATENT, HEADS * KVW))
    parts = 4
    width = COLS_HERE // parts

    def kernel(gram_ref, fresh_hbm, out_hbm, fresh_ref, base_ref, out_ref, sems):
        load = pltpu.make_async_copy(fresh_hbm, fresh_ref, sems.at[0])
        load.start()
        on_diagonal = lax.broadcasted_iota(jnp.int32, (TILE, TILE), 0) == lax.broadcasted_iota(
            jnp.int32, (TILE, TILE), 1
        )
        squares = jnp.zeros((TILE, TILE), F32)
        for k, (a, b) in enumerate(PAIRS):
            if a == b:
                squares = squares + jnp.where(on_diagonal, gram_ref[k].astype(F32), 0.0)
        squares = jnp.sum(jnp.sum(squares, axis=0, keepdims=True), axis=1, keepdims=True)
        norm = jnp.sqrt(squares) + norm_epsilon
        ratio, power = to_range(norm * norm)
        low_power = power.astype(BF16)
        for k, (a, b) in enumerate(PAIRS):
            block = gram_ref[k]
            base_ref[a * TILE : (a + 1) * TILE, b * TILE : (b + 1) * TILE] = block * low_power
            if a != b:
                base_ref[b * TILE : (b + 1) * TILE, a * TILE : (a + 1) * TILE] = block.T * low_power
        inv = 1.0 / ratio
        first = jnp.where(
            lax.broadcasted_iota(jnp.int32, (LATENT, LATENT), 0)
            == lax.broadcasted_iota(jnp.int32, (LATENT, LATENT), 1),
            poly_first,
            0.0,
        ).astype(F32)
        base = base_ref[...]
        poly = split(first + (poly_second * inv) * base.astype(F32) + (poly_third * inv * inv) * dot(base, base))
        inner = (inv * dot(base, product(poly, poly).astype(BF16))).astype(BF16)
        later = first + poly_second * inner.astype(F32) + poly_third * dot(inner, inner)
        high, low = split(product(split(later), poly))
        factor = update_scale / norm
        load.wait()
        stores = []
        for k in range(parts):
            at = slice(k * width, (k + 1) * width)
            fresh = fresh_ref[:, at]
            out_ref[:, at] = (dot(high, fresh) + dot(low, fresh)) * factor
            stores.append(pltpu.make_async_copy(out_ref.at[:, at], out_hbm.at[:, at], sems.at[1 + k]))
            stores[-1].start()
        for store in stores:
            store.wait()

    anywhere = pl.BlockSpec(memory_space=pl.ANY)
    return pl.pallas_call(
        kernel,
        in_specs=[IN_VMEM, anywhere],
        out_specs=anywhere,
        out_shape=jax.ShapeDtypeStruct((LATENT, COLS_HERE), F32),
        scratch_shapes=[
            pltpu.VMEM((LATENT, COLS_HERE), BF16),
            pltpu.VMEM((LATENT, LATENT), BF16),
            pltpu.VMEM((LATENT, COLS_HERE), F32),
            pltpu.SemaphoreType.DMA((1 + parts,)),
        ],
        name="update",
    )(gram, fresh)


def reduce_gram(gram):
    pieces = gram.reshape(NYX, -1, TILE)
    got = lax.all_to_all(pieces, YX, 0, 0, tiled=True)
    mine = jnp.sum(got.astype(F32), axis=0).astype(BF16)
    other = lax.ppermute(mine, "zh", [(0, 1), (1, 0)])
    mine = (mine.astype(F32) + other.astype(F32)).astype(BF16)
    full = lax.all_to_all(jnp.broadcast_to(mine[None], pieces.shape), YX, 0, 0, tiled=True)
    return full.reshape(gram.shape)


def pick(a, index):
    return lax.dynamic_index_in_dim(a, index, 0, keepdims=False)


STEPS_FIRST = (0, 6, 7, 1, 2)
STEPS_MIDDLE = (3, 4)
STEP_LAST = 5
STEP_OPENING = 6
ORDER = STEPS_FIRST + STEPS_MIDDLE + (STEP_LAST,)
HALF_Q = HD * QW // 2
HALF_V = HD * VDIM // 2


def pack(queries, grad_out, cuts):
    widths = [(q.stop - q.start, v.stop - v.start) for _, q, v in cuts]

    def kernel(queries_ref, grads_ref, *refs):
        n = len(cuts)
        here = lax.axis_index(DP)
        copies = []
        for k, (s, q, v) in enumerate(cuts):
            wide = widths[k][0]
            copies.append(
                pltpu.make_async_copy(
                    queries_ref.at[here ^ s, :, q], refs[k].at[:, :wide], refs[n].at[2 * k]
                )
            )
            copies.append(
                pltpu.make_async_copy(
                    grads_ref.at[here ^ s, :, v], refs[k].at[:, wide:], refs[n].at[2 * k + 1]
                )
            )
        for copy in copies:
            copy.start()
        for copy in copies:
            copy.wait()

    anywhere = pl.BlockSpec(memory_space=pl.ANY)
    return pl.pallas_call(
        kernel,
        in_specs=[anywhere, anywhere],
        out_specs=[IN_VMEM] * len(cuts),
        out_shape=[jax.ShapeDtypeStruct((SEQ, a + b), BF16) for a, b in widths],
        scratch_shapes=[pltpu.SemaphoreType.DMA((2 * len(cuts),))],
    )(queries, grad_out)


def send(chunk, s):
    return lax.ppermute(chunk, DP, [(k, k ^ s) for k in range(NDP)])


def inner_body(latent, rope_keys, queries, grad_out, key_value_up_weight, momentum):
    here = lax.axis_index(DP)
    halves = pack(
        queries,
        grad_out,
        [(STEP_OPENING, slice(k * HALF_Q, (k + 1) * HALF_Q), slice(k * HALF_V, (k + 1) * HALF_V)) for k in range(2)],
    )
    halves, queries, grad_out, latent, rope_keys = lax.optimization_barrier(
        (halves, queries, grad_out, latent, rope_keys)
    )
    others = [s for s in ORDER if s != STEP_OPENING]
    packed = pack(queries, grad_out, [(s, slice(0, HD * QW), slice(0, HD * VDIM)) for s in others])
    chunks = {s: (send(chunk, s) if s else chunk,) for s, chunk in zip(others, packed)}
    chunks[STEP_OPENING] = tuple(send(h, STEP_OPENING) for h in halves)
    at = ROWS * lax.axis_index(YX)
    rows = jnp.concatenate(
        [lax.dynamic_slice_in_dim(latent, at, ROWS, axis=1), lax.dynamic_slice_in_dim(rope_keys, at, ROWS, axis=1)],
        axis=2,
    )
    rows = lax.all_to_all(rows, DP, 0, 0, tiled=True)
    rows = jnp.stack([pick(rows, here ^ s) for s in ORDER])
    rows = lax.all_to_all(jnp.broadcast_to(rows[None], (NYX,) + rows.shape), YX, 0, 0, tiled=True)
    rows = rows.transpose(1, 0, 2, 3).reshape(NDP, SEQ, LATENT + ROPE)

    weight = key_value_up_weight[0]
    sofar = first_sequences(rows, weight, momentum[0], [chunks[s] for s in STEPS_FIRST])
    sofar, kv, last_rows, turned = middle_sequences(
        rows, weight, sofar, len(STEPS_FIRST), [chunks[s] for s in STEPS_MIDDLE]
    )
    fresh, gram = last_sequence(last_rows, turned, kv, sofar, chunks[STEP_LAST][0])
    step = update(reduce_gram(gram), fresh)
    return fresh[None], step[None]


def solution(mesh):
    fine = Mesh(mesh.devices.reshape(4, 2, 4, 4, 2), ("zl", "core", "y", "x", "zh"))
    heads = ("y", "x", "zh")
    placed = (
        P(None, DP, None),
        P(None, DP, None),
        P(None, DP, heads),
        P(None, DP, heads),
        P(DP, None, heads),
        P(DP, None, heads),
    )
    return jax.shard_map(
        inner_body,
        mesh=fine,
        in_specs=placed,
        out_specs=(P(DP, None, heads), P(DP, None, heads)),
        check_vma=False,
    )
```

```python
import math

import jax
import jax.numpy as jnp
from jax import lax
from jax.experimental import pallas as pl
from jax.experimental.pallas import tpu as pltpu
from jax.sharding import Mesh
from jax.sharding import PartitionSpec as P


LATENT = 512
HEADS = 128
NOPE = 128
ROPE = 64
VDIM = 128
SEQ = 128
HD = 4
QW = NOPE + ROPE
KVW = NOPE + VDIM
COLS_HERE = HD * KVW
TILE = 128
NT = LATENT // TILE
PAIRS = [(a, b) for a in range(NT) for b in range(a, NT)]

DP = ("zl", "core")
YX = ("y", "x")
NDP = 8
NYX = 16
ROWS = SEQ // NYX

poly_first = 3.4445
poly_second = -4.775
poly_third = 2.0315
norm_epsilon = 1e-07
decay_rate = 0.95

F32 = jnp.float32
BF16 = jnp.bfloat16
VMEM_LIMIT = 40 * 1024 * 1024


def contract_last(a, b):
    return lax.dot_general(a, b, (((1,), (1,)), ((), ())), preferred_element_type=F32)


def contract_first(a, b):
    return lax.dot_general(a, b, (((0,), (0,)), ((), ())), preferred_element_type=F32)


def up_project(rows, weight):
    return jnp.dot(rows[:, :LATENT], weight, preferred_element_type=F32).astype(BF16)


def attend(rows, kv, tokens):
    scale = 1.0 / math.sqrt(QW)
    key_at = lax.broadcasted_iota(jnp.int32, (SEQ, SEQ), 0)
    query_at = lax.broadcasted_iota(jnp.int32, (SEQ, SEQ), 1)
    allowed = key_at <= query_at
    queries, cots, scores, grad_probs = [], [], [], []
    for k in range(len(tokens)):
        at = slice(k * SEQ, (k + 1) * SEQ)
        for h in range(HD):
            keys = kv[at, h * KVW : h * KVW + NOPE]
            values = kv[at, h * KVW + NOPE : (h + 1) * KVW]
            query = tokens[k][:, h * QW : (h + 1) * QW]
            cot = tokens[k][:, HD * QW + h * VDIM : HD * QW + (h + 1) * VDIM]
            queries.append(query[:, :NOPE])
            cots.append(cot)
            scores.append(contract_last(jnp.concatenate([keys, rows[at, LATENT:]], axis=1), query))
            grad_probs.append(contract_last(values, cot))
    low, grads = [], []
    for score, grad_prob in zip(scores, grad_probs):
        score = jnp.where(allowed, score * scale, -jnp.inf)
        expd = jnp.exp(score - jnp.max(score, axis=0, keepdims=True))
        probs = expd * (1.0 / jnp.sum(expd, axis=0, keepdims=True))
        delta = jnp.sum(probs * grad_prob, axis=0, keepdims=True)
        low.append(probs.astype(BF16))
        grads.append((probs * (grad_prob - delta) * scale).astype(BF16))
    out = []
    for query, cot, probs, grad in zip(queries, cots, low, grads):
        out.append(jnp.dot(grad, query, preferred_element_type=F32).astype(BF16))
        out.append(jnp.dot(probs, cot, preferred_element_type=F32).astype(BF16))
    wide = 2 * HD
    return jnp.concatenate([jnp.concatenate(out[k * wide : (k + 1) * wide], axis=1) for k in range(len(tokens))], axis=0)


IN_VMEM = pl.BlockSpec(memory_space=pltpu.VMEM)
ROOMY = pltpu.CompilerParams(vmem_limit_bytes=VMEM_LIMIT)


def on_chip(a):
    return pltpu.with_memory_space_constraint(a, pltpu.VMEM)


def read_chunks(chunks, refs):
    out, at = [], 0
    for parts in chunks:
        got = [r[...] for r in refs[at : at + len(parts)]]
        at += len(parts)
        if len(parts) == 2:
            half = HD * QW // 2
            got = [jnp.concatenate([g[:, :half] for g in got] + [g[:, half:] for g in got], axis=1)]
        out.append(got[0])
    return out


def first_sequences(rows, weight, momentum, chunks):
    n = len(chunks)
    flat = [part for parts in chunks for part in parts]

    def kernel(rows_ref, weight_ref, mom_ref, *refs):
        here = rows_ref[:n].reshape(n * SEQ, LATENT + ROPE)
        dkv = attend(here, up_project(here, weight_ref[...]), read_chunks(chunks, refs))
        refs[-1][...] = decay_rate * mom_ref[...].astype(F32) + contract_first(here[:, :LATENT], dkv)

    return pl.pallas_call(
        kernel,
        in_specs=[IN_VMEM] * (3 + len(flat)),
        out_specs=IN_VMEM,
        out_shape=pltpu.VMEM((LATENT, COLS_HERE), F32),
        compiler_params=ROOMY,
        name="first_sequences",
    )(rows, weight, momentum, *flat)


def middle_sequences(rows, weight, sofar, first, chunks):
    n = len(chunks)
    flat = [part for parts in chunks for part in parts]

    def kernel(rows_ref, weight_ref, sofar_ref, *refs):
        out_ref, kv_ref, last_ref, turned_ref = refs[-4:]
        here = rows_ref[first:].reshape((n + 1) * SEQ, LATENT + ROPE)
        kv = up_project(here, weight_ref[...])
        kv_ref[...] = kv[n * SEQ :]
        last = here[n * SEQ :]
        last_ref[...] = last
        turned_ref[...] = last[:, :LATENT].T
        dkv = attend(here, kv, read_chunks(chunks, refs))
        out_ref[...] = sofar_ref[...] + contract_first(here[: n * SEQ, :LATENT], dkv)

    return pl.pallas_call(
        kernel,
        in_specs=[IN_VMEM] * (3 + len(flat)),
        out_specs=(IN_VMEM,) * 4,
        out_shape=(
            pltpu.VMEM((LATENT, COLS_HERE), F32),
            pltpu.VMEM((SEQ, COLS_HERE), BF16),
            pltpu.VMEM((SEQ, LATENT + ROPE), BF16),
            pltpu.VMEM((LATENT, SEQ), BF16),
        ),
        compiler_params=ROOMY,
        name="middle_sequences",
    )(rows, weight, on_chip(sofar), *flat)


def last_sequence(rows, turned, kv, sofar, chunk):
    half = LATENT // 2
    split_at = NT // 2

    def kernel(rows_ref, turned_ref, kv_ref, chunk_ref, sofar_ref, fresh_ref, gram_ref):
        dkv = attend(rows_ref[...], kv_ref[...], [chunk_ref[...]])
        fresh = (sofar_ref[...] + dot(turned_ref[...], dkv)).astype(BF16)
        fresh_ref[...] = fresh
        top = contract_last(fresh[:half], fresh).astype(BF16)
        low = contract_last(fresh[half:], fresh[half:]).astype(BF16)
        for k, (a, b) in enumerate(PAIRS):
            if a < split_at:
                gram_ref[k] = top[a * TILE : (a + 1) * TILE, b * TILE : (b + 1) * TILE]
            else:
                a, b = a - split_at, b - split_at
                gram_ref[k] = low[a * TILE : (a + 1) * TILE, b * TILE : (b + 1) * TILE]

    return pl.pallas_call(
        kernel,
        in_specs=[IN_VMEM] * 5,
        out_specs=(IN_VMEM, IN_VMEM),
        out_shape=(
            pltpu.VMEM((LATENT, COLS_HERE), BF16),
            pltpu.VMEM((len(PAIRS), TILE, TILE), BF16),
        ),
        compiler_params=ROOMY,
        name="last_sequence",
    )(*[on_chip(a) for a in (rows, turned, kv, chunk, sofar)])


def split(a):
    high = a.astype(BF16)
    return high, (a - high.astype(F32)).astype(BF16)


def product(a, b):
    d = lambda u, v: jnp.dot(u, v, preferred_element_type=F32)
    return d(a[0], b[0]) + (d(a[0], b[1]) + d(a[1], b[0]))


def to_range(t):
    p = jnp.full_like(t, 2.0**64)
    for edge in (-48, -16, 16, 48, 80):
        p = jnp.where(t >= 2.0**edge, 2.0 ** -(edge + 16), p)
    return t * p, p


def dot(a, b):
    return jnp.dot(a, b, preferred_element_type=F32)


def update(gram, fresh):
    update_scale = 0.2 * math.sqrt(max(LATENT, HEADS * KVW))
    parts = 4
    width = COLS_HERE // parts

    def kernel(gram_ref, fresh_ref, out_hbm, momentum_hbm, base_ref, out_ref, sems):
        stores = [pltpu.make_async_copy(fresh_ref, momentum_hbm, sems.at[parts])]
        stores[0].start()
        on_diagonal = lax.broadcasted_iota(jnp.int32, (TILE, TILE), 0) == lax.broadcasted_iota(
            jnp.int32, (TILE, TILE), 1
        )
        squares = jnp.zeros((TILE, TILE), F32)
        for k, (a, b) in enumerate(PAIRS):
            if a == b:
                squares = squares + jnp.where(on_diagonal, gram_ref[k].astype(F32), 0.0)
        squares = jnp.sum(jnp.sum(squares, axis=0, keepdims=True), axis=1, keepdims=True)
        norm = jnp.sqrt(squares) + norm_epsilon
        ratio, power = to_range(norm * norm)
        low_power = power.astype(BF16)
        for k, (a, b) in enumerate(PAIRS):
            block = gram_ref[k]
            base_ref[a * TILE : (a + 1) * TILE, b * TILE : (b + 1) * TILE] = block * low_power
            if a != b:
                base_ref[b * TILE : (b + 1) * TILE, a * TILE : (a + 1) * TILE] = block.T * low_power
        inv = 1.0 / ratio
        first = jnp.where(
            lax.broadcasted_iota(jnp.int32, (LATENT, LATENT), 0)
            == lax.broadcasted_iota(jnp.int32, (LATENT, LATENT), 1),
            poly_first,
            0.0,
        ).astype(F32)
        base = base_ref[...]
        poly = split(first + (poly_second * inv) * base.astype(F32) + (poly_third * inv * inv) * dot(base, base))
        inner = (inv * dot(base, product(poly, poly).astype(BF16))).astype(BF16)
        later = first + poly_second * inner.astype(F32) + poly_third * dot(inner, inner)
        high, low = split(product(split(later), poly))
        factor = update_scale / norm
        for k in range(parts):
            at = slice(k * width, (k + 1) * width)
            fresh = fresh_ref[:, at]
            out_ref[:, at] = (dot(high, fresh) + dot(low, fresh)) * factor
            stores.append(pltpu.make_async_copy(out_ref.at[:, at], out_hbm.at[:, at], sems.at[k]))
            stores[-1].start()
        for store in stores:
            store.wait()

    anywhere = pl.BlockSpec(memory_space=pl.ANY)
    return pl.pallas_call(
        kernel,
        in_specs=[IN_VMEM, IN_VMEM],
        out_specs=(anywhere, anywhere),
        out_shape=(
            jax.ShapeDtypeStruct((LATENT, COLS_HERE), F32),
            jax.ShapeDtypeStruct((LATENT, COLS_HERE), BF16),
        ),
        scratch_shapes=[
            pltpu.VMEM((LATENT, LATENT), BF16),
            pltpu.VMEM((LATENT, COLS_HERE), F32),
            pltpu.SemaphoreType.DMA((parts + 1,)),
        ],
        compiler_params=ROOMY,
        name="update",
    )(on_chip(gram), on_chip(fresh))


def reduce_gram(gram):
    pieces = gram.reshape(NYX, -1, TILE)
    got = lax.all_to_all(pieces, YX, 0, 0, tiled=True)
    mine = jnp.sum(got.astype(F32), axis=0).astype(BF16)
    other = lax.ppermute(mine, "zh", [(0, 1), (1, 0)])
    mine = (mine.astype(F32) + other.astype(F32)).astype(BF16)
    full = lax.all_to_all(jnp.broadcast_to(mine[None], pieces.shape), YX, 0, 0, tiled=True)
    return full.reshape(gram.shape)


def pick(a, index):
    return lax.dynamic_index_in_dim(a, index, 0, keepdims=False)


STEPS_FIRST = (0, 6, 7, 1, 2)
STEPS_MIDDLE = (3, 4)
STEP_LAST = 5
STEP_OPENING = 6
ORDER = STEPS_FIRST + STEPS_MIDDLE + (STEP_LAST,)
HALF_Q = HD * QW // 2
HALF_V = HD * VDIM // 2


def pack(queries, grad_out, cuts):
    widths = [(q.stop - q.start, v.stop - v.start) for _, q, v in cuts]

    def kernel(queries_ref, grads_ref, *refs):
        n = len(cuts)
        here = lax.axis_index(DP)
        copies = []
        for k, (s, q, v) in enumerate(cuts):
            wide = widths[k][0]
            copies.append(
                pltpu.make_async_copy(
                    queries_ref.at[here ^ s, :, q], refs[k].at[:, :wide], refs[n].at[2 * k]
                )
            )
            copies.append(
                pltpu.make_async_copy(
                    grads_ref.at[here ^ s, :, v], refs[k].at[:, wide:], refs[n].at[2 * k + 1]
                )
            )
        for copy in copies:
            copy.start()
        for copy in copies:
            copy.wait()

    anywhere = pl.BlockSpec(memory_space=pl.ANY)
    return pl.pallas_call(
        kernel,
        in_specs=[anywhere, anywhere],
        out_specs=[IN_VMEM] * len(cuts),
        out_shape=[jax.ShapeDtypeStruct((SEQ, a + b), BF16) for a, b in widths],
        scratch_shapes=[pltpu.SemaphoreType.DMA((2 * len(cuts),))],
    )(queries, grad_out)


def send(chunk, s):
    return lax.ppermute(chunk, DP, [(k, k ^ s) for k in range(NDP)])


def inner_body(latent, rope_keys, queries, grad_out, key_value_up_weight, momentum):
    here = lax.axis_index(DP)
    halves = pack(
        queries,
        grad_out,
        [(STEP_OPENING, slice(k * HALF_Q, (k + 1) * HALF_Q), slice(k * HALF_V, (k + 1) * HALF_V)) for k in range(2)],
    )
    halves, queries, grad_out, latent, rope_keys = lax.optimization_barrier(
        (halves, queries, grad_out, latent, rope_keys)
    )
    others = [s for s in ORDER if s != STEP_OPENING]
    packed = pack(queries, grad_out, [(s, slice(0, HD * QW), slice(0, HD * VDIM)) for s in others])
    chunks = {s: (send(chunk, s) if s else chunk,) for s, chunk in zip(others, packed)}
    chunks[STEP_OPENING] = tuple(send(h, STEP_OPENING) for h in halves)
    at = ROWS * lax.axis_index(YX)
    rows = jnp.concatenate(
        [lax.dynamic_slice_in_dim(latent, at, ROWS, axis=1), lax.dynamic_slice_in_dim(rope_keys, at, ROWS, axis=1)],
        axis=2,
    )
    rows = lax.all_to_all(rows, DP, 0, 0, tiled=True)
    rows = jnp.stack([pick(rows, here ^ s) for s in ORDER])
    rows = lax.all_to_all(jnp.broadcast_to(rows[None], (NYX,) + rows.shape), YX, 0, 0, tiled=True)
    rows = rows.transpose(1, 0, 2, 3).reshape(NDP, SEQ, LATENT + ROPE)

    weight = key_value_up_weight[0]
    sofar = first_sequences(rows, weight, momentum[0], [chunks[s] for s in STEPS_FIRST])
    sofar, kv, last_rows, turned = middle_sequences(
        rows, weight, sofar, len(STEPS_FIRST), [chunks[s] for s in STEPS_MIDDLE]
    )
    fresh, gram = last_sequence(last_rows, turned, kv, sofar, chunks[STEP_LAST][0])
    step, fresh = update(reduce_gram(gram), fresh)
    return fresh[None], step[None]


def solution(mesh):
    fine = Mesh(mesh.devices.reshape(4, 2, 4, 4, 2), ("zl", "core", "y", "x", "zh"))
    heads = ("y", "x", "zh")
    placed = (
        P(None, DP, None),
        P(None, DP, None),
        P(None, DP, heads),
        P(None, DP, heads),
        P(DP, None, heads),
        P(DP, None, heads),
    )
    return jax.shard_map(
        inner_body,
        mesh=fine,
        in_specs=placed,
        out_specs=(P(DP, None, heads), P(DP, None, heads)),
        check_vma=False,
    )
```

```python
import math

import jax
import jax.numpy as jnp
from jax import lax
from jax.experimental import pallas as pl
from jax.experimental.pallas import tpu as pltpu
from jax.sharding import Mesh
from jax.sharding import PartitionSpec as P


LATENT = 512
HEADS = 128
NOPE = 128
ROPE = 64
VDIM = 128
SEQ = 128
HD = 4
QW = NOPE + ROPE
KVW = NOPE + VDIM
COLS_HERE = HD * KVW
TILE = 128
NT = LATENT // TILE
PAIRS = [(a, b) for a in range(NT) for b in range(a, NT)]

DP = ("zl", "core")
YX = ("y", "x")
NDP = 8
NYX = 16
ROWS = SEQ // NYX

poly_first = 3.4445
poly_second = -4.775
poly_third = 2.0315
norm_epsilon = 1e-07
decay_rate = 0.95

F32 = jnp.float32
BF16 = jnp.bfloat16
VMEM_LIMIT = 40 * 1024 * 1024


def contract_last(a, b):
    return lax.dot_general(a, b, (((1,), (1,)), ((), ())), preferred_element_type=F32)


def contract_first(a, b):
    return lax.dot_general(a, b, (((0,), (0,)), ((), ())), preferred_element_type=F32)


def up_project(rows, weight):
    return jnp.dot(rows[:, :LATENT], weight, preferred_element_type=F32).astype(BF16)


def attend(rows, kv, tokens, heads=HD):
    scale = 1.0 / math.sqrt(QW)
    key_at = lax.broadcasted_iota(jnp.int32, (SEQ, SEQ), 0)
    query_at = lax.broadcasted_iota(jnp.int32, (SEQ, SEQ), 1)
    allowed = key_at <= query_at
    queries, cots, scores, grad_probs = [], [], [], []
    for k in range(len(tokens)):
        at = slice(k * SEQ, (k + 1) * SEQ)
        for h in range(heads):
            keys = kv[at, h * KVW : h * KVW + NOPE]
            values = kv[at, h * KVW + NOPE : (h + 1) * KVW]
            query = tokens[k][:, h * QW : (h + 1) * QW]
            cot = tokens[k][:, heads * QW + h * VDIM : heads * QW + (h + 1) * VDIM]
            queries.append(query[:, :NOPE])
            cots.append(cot)
            scores.append(contract_last(jnp.concatenate([keys, rows[at, LATENT:]], axis=1), query))
            grad_probs.append(contract_last(values, cot))
    low, grads = [], []
    for score, grad_prob in zip(scores, grad_probs):
        score = jnp.where(allowed, score * scale, -jnp.inf)
        expd = jnp.exp(score - jnp.max(score, axis=0, keepdims=True))
        probs = expd * (1.0 / jnp.sum(expd, axis=0, keepdims=True))
        delta = jnp.sum(probs * grad_prob, axis=0, keepdims=True)
        low.append(probs.astype(BF16))
        grads.append((probs * (grad_prob - delta) * scale).astype(BF16))
    out = []
    for query, cot, probs, grad in zip(queries, cots, low, grads):
        out.append(jnp.dot(grad, query, preferred_element_type=F32).astype(BF16))
        out.append(jnp.dot(probs, cot, preferred_element_type=F32).astype(BF16))
    wide = 2 * heads
    return jnp.concatenate([jnp.concatenate(out[k * wide : (k + 1) * wide], axis=1) for k in range(len(tokens))], axis=0)


IN_VMEM = pl.BlockSpec(memory_space=pltpu.VMEM)
ROOMY = pltpu.CompilerParams(vmem_limit_bytes=VMEM_LIMIT)


def on_chip(a):
    return pltpu.with_memory_space_constraint(a, pltpu.VMEM)


def read_chunks(chunks, refs):
    out, at = [], 0
    for parts in chunks:
        got = [r[...] for r in refs[at : at + len(parts)]]
        at += len(parts)
        if len(parts) == 2:
            half = HD * QW // 2
            got = [jnp.concatenate([g[:, :half] for g in got] + [g[:, half:] for g in got], axis=1)]
        out.append(got[0])
    return out


def first_sequences(rows, weight, momentum, chunks):
    n = len(chunks)
    flat = [part for parts in chunks for part in parts]

    def kernel(rows_ref, weight_ref, mom_ref, *refs):
        here = rows_ref[:n].reshape(n * SEQ, LATENT + ROPE)
        dkv = attend(here, up_project(here, weight_ref[...]), read_chunks(chunks, refs))
        refs[-1][...] = decay_rate * mom_ref[...].astype(F32) + contract_first(here[:, :LATENT], dkv)

    return pl.pallas_call(
        kernel,
        in_specs=[IN_VMEM] * (3 + len(flat)),
        out_specs=IN_VMEM,
        out_shape=pltpu.VMEM((LATENT, COLS_HERE), F32),
        compiler_params=ROOMY,
        name="first_sequences",
    )(rows, weight, momentum, *flat)


def middle_sequences(rows, weight, sofar, first, chunks):
    n = len(chunks)
    flat = [part for parts in chunks for part in parts]

    def kernel(rows_ref, weight_ref, sofar_ref, *refs):
        out_ref, kv_ref, last_ref, turned_ref = refs[-4:]
        here = rows_ref[first:].reshape((n + 1) * SEQ, LATENT + ROPE)
        kv = up_project(here, weight_ref[...])
        kv_ref[...] = kv[n * SEQ :]
        last = here[n * SEQ :]
        last_ref[...] = last
        turned_ref[...] = last[:, :LATENT].T
        dkv = attend(here, kv, read_chunks(chunks, refs))
        out_ref[...] = sofar_ref[...] + contract_first(here[: n * SEQ, :LATENT], dkv)

    return pl.pallas_call(
        kernel,
        in_specs=[IN_VMEM] * (3 + len(flat)),
        out_specs=(IN_VMEM,) * 4,
        out_shape=(
            pltpu.VMEM((LATENT, COLS_HERE), F32),
            pltpu.VMEM((SEQ, COLS_HERE), BF16),
            pltpu.VMEM((SEQ, LATENT + ROPE), BF16),
            pltpu.VMEM((LATENT, SEQ), BF16),
        ),
        compiler_params=ROOMY,
        name="middle_sequences",
    )(rows, weight, on_chip(sofar), *flat)


def last_sequence(rows, turned, kv, sofar, chunk, part, gram_before):
    half = LATENT // 2
    split_at = NT // 2
    cols = COLS_HERE // 2
    at = slice(part * cols, (part + 1) * cols)

    def kernel(rows_ref, turned_ref, kv_ref, chunk_ref, sofar_ref, *refs):
        dkv = attend(rows_ref[...], kv_ref[:, at], [chunk_ref[...]], HD // 2)
        fresh = (sofar_ref[:, at] + dot(turned_ref[...], dkv)).astype(BF16)
        refs[-2][...] = fresh
        top = contract_last(fresh[:half], fresh)
        low = contract_last(fresh[half:], fresh[half:])
        if part == 0:
            refs[-1][:half, :] = top
            refs[-1][half:, :half] = low
            return
        top = (refs[0][:half, :] + top).astype(BF16)
        low = (refs[0][half:, :half] + low).astype(BF16)
        for k, (a, b) in enumerate(PAIRS):
            if a < split_at:
                refs[-1][k] = top[a * TILE : (a + 1) * TILE, b * TILE : (b + 1) * TILE]
            else:
                a, b = a - split_at, b - split_at
                refs[-1][k] = low[a * TILE : (a + 1) * TILE, b * TILE : (b + 1) * TILE]

    args = (rows, turned, kv, chunk, sofar) + ((gram_before,) if part else ())
    return pl.pallas_call(
        kernel,
        in_specs=[IN_VMEM] * len(args),
        out_specs=(IN_VMEM, IN_VMEM),
        out_shape=(
            pltpu.VMEM((LATENT, cols), BF16),
            pltpu.VMEM((len(PAIRS), TILE, TILE), BF16) if part else pltpu.VMEM((LATENT, LATENT), F32),
        ),
        compiler_params=ROOMY,
    )(*[on_chip(a) for a in args])


def split(a):
    high = a.astype(BF16)
    return high, (a - high.astype(F32)).astype(BF16)


def product(a, b):
    d = lambda u, v: jnp.dot(u, v, preferred_element_type=F32)
    return d(a[0], b[0]) + (d(a[0], b[1]) + d(a[1], b[0]))


def to_range(t):
    p = jnp.full_like(t, 2.0**64)
    for edge in (-48, -16, 16, 48, 80):
        p = jnp.where(t >= 2.0**edge, 2.0 ** -(edge + 16), p)
    return t * p, p


def dot(a, b):
    return jnp.dot(a, b, preferred_element_type=F32)


def update(gram, fresh_halves):
    update_scale = 0.2 * math.sqrt(max(LATENT, HEADS * KVW))
    parts = 4
    width = COLS_HERE // parts

    cols = COLS_HERE // 2

    def kernel(gram_ref, fresh0_ref, fresh1_ref, out_hbm, momentum_hbm, base_ref, out_ref, sems):
        halves = (fresh0_ref, fresh1_ref)
        stores = [
            pltpu.make_async_copy(half, momentum_hbm.at[:, k * cols : (k + 1) * cols], sems.at[parts + k])
            for k, half in enumerate(halves)
        ]
        for store in stores:
            store.start()
        on_diagonal = lax.broadcasted_iota(jnp.int32, (TILE, TILE), 0) == lax.broadcasted_iota(
            jnp.int32, (TILE, TILE), 1
        )
        squares = jnp.zeros((TILE, TILE), F32)
        for k, (a, b) in enumerate(PAIRS):
            if a == b:
                squares = squares + jnp.where(on_diagonal, gram_ref[k].astype(F32), 0.0)
        squares = jnp.sum(jnp.sum(squares, axis=0, keepdims=True), axis=1, keepdims=True)
        norm = jnp.sqrt(squares) + norm_epsilon
        ratio, power = to_range(norm * norm)
        low_power = power.astype(BF16)
        for k, (a, b) in enumerate(PAIRS):
            block = gram_ref[k]
            base_ref[a * TILE : (a + 1) * TILE, b * TILE : (b + 1) * TILE] = block * low_power
            if a != b:
                base_ref[b * TILE : (b + 1) * TILE, a * TILE : (a + 1) * TILE] = block.T * low_power
        inv = 1.0 / ratio
        first = jnp.where(
            lax.broadcasted_iota(jnp.int32, (LATENT, LATENT), 0)
            == lax.broadcasted_iota(jnp.int32, (LATENT, LATENT), 1),
            poly_first,
            0.0,
        ).astype(F32)
        base = base_ref[...]
        poly = split(first + (poly_second * inv) * base.astype(F32) + (poly_third * inv * inv) * dot(base, base))
        square = dot(poly[0], poly[0]) + 2.0 * dot(poly[0], poly[1])
        inner = (inv * dot(base, square.astype(BF16))).astype(BF16)
        later = first + poly_second * inner.astype(F32) + poly_third * dot(inner, inner)
        high, low = split(product(split(later), poly))
        factor = update_scale / norm
        for k in range(parts):
            at = slice(k * width, (k + 1) * width)
            fresh = halves[k * width // cols][:, k * width % cols : k * width % cols + width]
            out_ref[:, at] = (dot(high, fresh) + dot(low, fresh)) * factor
            stores.append(pltpu.make_async_copy(out_ref.at[:, at], out_hbm.at[:, at], sems.at[k]))
            stores[-1].start()
        for store in stores:
            store.wait()

    anywhere = pl.BlockSpec(memory_space=pl.ANY)
    return pl.pallas_call(
        kernel,
        in_specs=[IN_VMEM] * 3,
        out_specs=(anywhere, anywhere),
        out_shape=(
            jax.ShapeDtypeStruct((LATENT, COLS_HERE), F32),
            jax.ShapeDtypeStruct((LATENT, COLS_HERE), BF16),
        ),
        scratch_shapes=[
            pltpu.VMEM((LATENT, LATENT), BF16),
            pltpu.VMEM((LATENT, COLS_HERE), F32),
            pltpu.SemaphoreType.DMA((parts + 2,)),
        ],
        compiler_params=ROOMY,
        name="update",
    )(on_chip(gram), *[on_chip(half) for half in fresh_halves])


def reduce_gram(gram):
    pieces = gram.reshape(NYX, -1, TILE)
    got = lax.all_to_all(pieces, YX, 0, 0, tiled=True)
    mine = jnp.sum(got.astype(F32), axis=0).astype(BF16)
    other = lax.ppermute(mine, "zh", [(0, 1), (1, 0)])
    mine = (mine.astype(F32) + other.astype(F32)).astype(BF16)
    full = lax.all_to_all(jnp.broadcast_to(mine[None], pieces.shape), YX, 0, 0, tiled=True)
    return full.reshape(gram.shape)


def pick(a, index):
    return lax.dynamic_index_in_dim(a, index, 0, keepdims=False)


STEPS_FIRST = (0, 6, 7, 1, 2)
STEPS_MIDDLE = (3, 4)
STEP_LAST = 5
STEP_OPENING = 6
HALVED = (STEP_OPENING, STEP_LAST)
ORDER = STEPS_FIRST + STEPS_MIDDLE + (STEP_LAST,)
HALF_Q = HD * QW // 2
HALF_V = HD * VDIM // 2


def pack(queries, grad_out, cuts):
    widths = [(q.stop - q.start, v.stop - v.start) for _, q, v in cuts]

    def kernel(queries_ref, grads_ref, *refs):
        n = len(cuts)
        here = lax.axis_index(DP)
        copies = []
        for k, (s, q, v) in enumerate(cuts):
            wide = widths[k][0]
            copies.append(
                pltpu.make_async_copy(
                    queries_ref.at[here ^ s, :, q], refs[k].at[:, :wide], refs[n].at[2 * k]
                )
            )
            copies.append(
                pltpu.make_async_copy(
                    grads_ref.at[here ^ s, :, v], refs[k].at[:, wide:], refs[n].at[2 * k + 1]
                )
            )
        for copy in copies:
            copy.start()
        for copy in copies:
            copy.wait()

    anywhere = pl.BlockSpec(memory_space=pl.ANY)
    return pl.pallas_call(
        kernel,
        in_specs=[anywhere, anywhere],
        out_specs=[IN_VMEM] * len(cuts),
        out_shape=[jax.ShapeDtypeStruct((SEQ, a + b), BF16) for a, b in widths],
        scratch_shapes=[pltpu.SemaphoreType.DMA((2 * len(cuts),))],
    )(queries, grad_out)


def send(chunk, s):
    return lax.ppermute(chunk, DP, [(k, k ^ s) for k in range(NDP)])


def inner_body(latent, rope_keys, queries, grad_out, key_value_up_weight, momentum):
    here = lax.axis_index(DP)
    in_halves = lambda s: [
        (s, slice(k * HALF_Q, (k + 1) * HALF_Q), slice(k * HALF_V, (k + 1) * HALF_V)) for k in range(2)
    ]
    opening = pack(queries, grad_out, in_halves(STEP_OPENING))
    opening, queries, grad_out, latent, rope_keys = lax.optimization_barrier(
        (opening, queries, grad_out, latent, rope_keys)
    )
    others = [s for s in ORDER if s not in HALVED]
    cuts = [(s, slice(0, HD * QW), slice(0, HD * VDIM)) for s in others] + in_halves(STEP_LAST)
    packed = pack(queries, grad_out, cuts)
    chunks = {s: (send(chunk, s) if s else chunk,) for s, chunk in zip(others, packed)}
    for s, halves in zip(HALVED, (opening, packed[-2:])):
        chunks[s] = tuple(send(h, s) for h in halves)
    at = ROWS * lax.axis_index(YX)
    rows = jnp.concatenate(
        [lax.dynamic_slice_in_dim(latent, at, ROWS, axis=1), lax.dynamic_slice_in_dim(rope_keys, at, ROWS, axis=1)],
        axis=2,
    )
    rows = lax.all_to_all(rows, DP, 0, 0, tiled=True)
    rows = jnp.stack([pick(rows, here ^ s) for s in ORDER])
    rows = lax.all_to_all(jnp.broadcast_to(rows[None], (NYX,) + rows.shape), YX, 0, 0, tiled=True)
    rows = rows.transpose(1, 0, 2, 3).reshape(NDP, SEQ, LATENT + ROPE)

    weight = key_value_up_weight[0]
    sofar = first_sequences(rows, weight, momentum[0], [chunks[s] for s in STEPS_FIRST])
    sofar, kv, last_rows, turned = middle_sequences(
        rows, weight, sofar, len(STEPS_FIRST), [chunks[s] for s in STEPS_MIDDLE]
    )
    fresh, gram = [], None
    for part, chunk in enumerate(chunks[STEP_LAST]):
        made, gram = last_sequence(last_rows, turned, kv, sofar, chunk, part, gram)
        fresh.append(made)
    step, fresh = update(reduce_gram(gram), fresh)
    return fresh[None], step[None]


def solution(mesh):
    fine = Mesh(mesh.devices.reshape(4, 2, 4, 4, 2), ("zl", "core", "y", "x", "zh"))
    heads = ("y", "x", "zh")
    placed = (
        P(None, DP, None),
        P(None, DP, None),
        P(None, DP, heads),
        P(None, DP, heads),
        P(DP, None, heads),
        P(DP, None, heads),
    )
    return jax.shard_map(
        inner_body,
        mesh=fine,
        in_specs=placed,
        out_specs=(P(DP, None, heads), P(DP, None, heads)),
        check_vma=False,
    )
```
